1024 devices in a mesh: grp: 16 (over x, y_hi, core), qb: 64 (over z, y_lo).
Axes of the slice: x: 4, y: 4 (y_hi: 2, y_lo: 2; y = y_hi * 2 + y_lo), z: 32, core: 2. Of those that a mesh axis runs over, the one named last changes fastest.
Arguments:
- amplitudes: float32 [2, 134217728], P(None, ('grp', 'qb')), may hold values from -6 to 6
- layer_gates: float32 [4, 2, 128, 128], replicated, may hold values from -0.375 to 0.375
- cross_gates: float32 [2, 2, 4, 4], replicated, may hold values from -2 to 2
Outputs:
- final_state: float32 [2, 134217728], P(None, ('grp', 'qb'))
The draws below stay inside these ranges and needn't reach their ends.
All inputs are finite; a program needn't handle non-finite values.
Results may differ from the reference program's by a relative error of at most 0.000084.
Values sent between devices are 32-bit elements; how exact they have to be, the bound alone decides.
A program may use at most 32 MiB of HBM per device.

```python
import jax
import jax.numpy as jnp
from jax import lax

LOC = 131072
GATE = 128
AMPS = 134217728
N_GRP = 16
N_QB = 64


def shard_levels(own_key, extent, pieces, smallest, high):
    loudness = 1.0
    for axis_at, blocks in pieces:
        heights = jax.random.uniform(jax.random.fold_in(jax.random.fold_in(own_key, 6), axis_at), (blocks,), jnp.float32, smallest / len(pieces), high / len(pieces))
        loudness = loudness * jnp.repeat(jnp.exp(heights), extent[axis_at] // blocks).reshape((-1,) + (1,) * (len(extent) - 1 - axis_at))
    return loudness


def scatter_about(rng, dims, deviation, most, cuts=(), dtype=jnp.bfloat16):
    values = jax.random.normal(rng, dims, jnp.float32) * deviation
    if len(cuts) > 0:
        values = shard_levels(rng, dims, cuts, -0.22, 0.18) * values
    return jnp.clip(values, min=-most, max=most).astype(dtype)


def setup_inputs(seed: int = 0) -> dict:
    splits = jax.random.split(jax.random.key(seed), 4)
    amplitudes = scatter_about(splits[0], (2, AMPS), 1.0, 6.0, ((1, 1024),), jnp.float32)
    layer_gates = scatter_about(splits[1], (4, 2, GATE, GATE), (2 * GATE) ** -0.5, 0.375, (), jnp.float32)
    cross_gates = scatter_about(splits[2], (2, 2, 4, 4), 8 ** -0.5, 2.0, (), jnp.float32)
    return dict(amplitudes=amplitudes, layer_gates=layer_gates, cross_gates=cross_gates)


def complex_mix(form, matrix, vector):
    precise = lax.Precision.HIGHEST
    real_part = jnp.einsum(form, matrix[0], vector[0], precision=precise) - jnp.einsum(form, matrix[1], vector[1], precision=precise)
    imag_part = jnp.einsum(form, matrix[0], vector[1], precision=precise) + jnp.einsum(form, matrix[1], vector[0], precision=precise)
    return jnp.stack([real_part, imag_part])


def apply_high(amplitudes, matrix):
    blocks = amplitudes.reshape(2, N_GRP * N_QB, GATE, LOC // GATE)
    return complex_mix("kj,ajb->akb", matrix, blocks).reshape(2, -1)


def apply_low(amplitudes, matrix):
    blocks = amplitudes.reshape(2, -1, GATE)
    return complex_mix("kj,aj->ak", matrix, blocks).reshape(2, -1)


def reference(amplitudes, layer_gates, cross_gates):
    section_one = apply_high(amplitudes, layer_gates[0])
    section_two = apply_low(section_one, layer_gates[1])
    swapped = section_two.reshape(2, N_GRP, N_QB, N_QB, LOC // N_QB)
    swapped = jnp.transpose(swapped, (0, 1, 3, 2, 4)).reshape(2, -1)
    section_three = apply_high(swapped, layer_gates[2])
    section_four = apply_low(section_three, layer_gates[3])
    lower_view = section_four.reshape(2, N_GRP // 4, 4, N_QB * LOC)
    section_five = complex_mix("kj,ajb->akb", cross_gates[0], lower_view).reshape(2, -1)
    upper_view = section_five.reshape(2, 4, -1)
    return complex_mix("kj,jb->kb", cross_gates[1], upper_view).reshape(2, -1)
```

```python
import functools

import jax
import jax.numpy as jnp
from jax import lax
from jax.experimental import pallas as pl
from jax.experimental.pallas import tpu as pltpu
from jax.sharding import PartitionSpec as P

MESH = pl.DeviceIdType.MESH
GATE = 128
NZ = 32
PARTS = 3
MIX_AT = 2
TURN_AT = (4, 5)
LATE_FROM = 7
BACK_AT = (17, 18)
BACK_MIX_AT = 21
HIGHEST = lax.Precision.HIGHEST


def ranges(low, high, parts):
    count = high - low + 1
    parts = min(parts, count)
    edges = [low + count * i // parts for i in range(parts + 1)]
    return [(edges[i], edges[i + 1] - 1) for i in reversed(range(parts))]


def kernel(groups, x_hbm, gates_hbm, cross, out_ref, first_x, late_x, gates, rep, turn,
           first_pre, late_pre, first_recv, late_recv, first_post, late_post, first_res, late_mixed, first_out, late_out,
           mix_in, mix_out, ssem, rsem, mix_s, mix_r, local_sem):
    g = lax.axis_index("grp")
    q = lax.axis_index("qb")
    z, y = q // 2, q % 2
    up, down = lax.rem(z + 1, NZ), lax.rem(z + NZ - 1, NZ)
    near = (up, down)

    barrier = pltpu.get_barrier_semaphore()

    def greet(to_g, to_q):
        pl.semaphore_signal(barrier, inc=1, device_id=(to_g, to_q), device_id_type=MESH)

    for zz in near:
        for yy in (0, 1):
            greet(g, zz * 2 + yy)
    greet(g, z * 2 + 1 - y)

    def greet_group(i, c):
        greet(lax.rem(g + i, groups), q)
        return c

    lax.fori_loop(1, groups, greet_group, 0)

    load_gates = pltpu.make_async_copy(gates_hbm, gates, local_sem.at[0])
    load_first = pltpu.make_async_copy(x_hbm.at[:, pl.ds(0, 8), :], first_x, local_sem.at[1])
    load_late = pltpu.make_async_copy(x_hbm.at[:, pl.ds(8, 8), :], late_x, local_sem.at[2])
    load_gates.start()
    load_first.start()
    load_late.start()

    def real_form(index, place):
        re, im = gates[index, 0], gates[index, 1]
        rep[place, 0:GATE, 0:GATE] = re
        rep[place, 0:GATE, GATE:] = -im
        rep[place, GATE:, 0:GATE] = im
        rep[place, GATE:, GATE:] = re

    def rows(ref, r, part):
        return ref[pl.ds(r * 2 + part, GATE, stride=8), :]

    def high_gate(place, columns):
        return jnp.dot(rep[place], columns, precision=HIGHEST, preferred_element_type=jnp.float32)

    def low_gate(stacked):
        return lax.dot_general(stacked, turn[...], (((1,), (1,)), ((), ())), precision=HIGHEST,
                               preferred_element_type=jnp.float32)

    def columns_of(ref, pair):
        return jnp.concatenate(
            [jnp.concatenate([rows(ref, r, part) for r in pair], axis=1) for part in (0, 1)], axis=0)

    def put(ref, base, pair, value):
        for i, r in enumerate(pair):
            for part in (0, 1):
                ref[pl.ds(base + r * 2 + part, GATE, stride=8), :] = value[
                    part * GATE:(part + 1) * GATE, i * GATE:(i + 1) * GATE]

    flat = (1024, GATE)
    pairs = ((0, 1), (2, 3))

    sems = {}

    def sem_of(key):
        return sems.setdefault(key, len(sems))

    sent = []

    def send(key, src, dst, to_g, to_q):
        k = sem_of(key)
        copy = pltpu.make_async_remote_copy(src_ref=src, dst_ref=dst, send_sem=ssem.at[k], recv_sem=rsem.at[k],
                                            device_id=(to_g, to_q), device_id_type=MESH)
        copy.start()
        sent.append(copy)

    def arrived(key, src, dst):
        k = sem_of(key)
        pltpu.make_async_remote_copy(src_ref=src, dst_ref=dst, send_sem=ssem.at[k], recv_sem=rsem.at[k],
                                     device_id=(g, q), device_id_type=MESH).wait_recv()

    first_n = (16, 15)

    def first_start(way, low, high):
        return low if way == 0 else 15 - high

    def first_own(way, low, high, cross_y):
        n = high - low + 1
        to_y = 1 - y if cross_y else y
        at = z + low + 1 if way == 0 else z + NZ - high - 1
        send(("f", way, 1, low, cross_y), first_pre.at[pl.ds(at, n), to_y],
             first_recv.at[way, 0, pl.ds(first_start(way, low, high), n), y], g, near[way] * 2 + to_y)

    def first_pass(way, step, low, high):
        n = high - low + 1
        send(("f", way, step, low, 0), first_recv.at[way, step - 2, pl.ds(first_start(way, low + 1, high + 1), n)],
             first_recv.at[way, step - 1, pl.ds(first_start(way, low, high), n)], g, near[way] * 2 + y)

    def first_ranges(way, step):
        return ranges(0, first_n[way] - step, PARTS) if step <= first_n[way] else []

    first_seen = set()

    def first_wait(way, step, low, high):
        if (way, step, low) in first_seen:
            return
        first_seen.add((way, step, low))
        n = high - low + 1
        at = first_start(way, low, high)
        if step == 1:
            for cross_y in (0, 1):
                from_y = 1 - y if cross_y else y
                arrived(("f", way, 1, low, cross_y), first_pre.at[pl.ds(0, n), 0],
                        first_recv.at[way, 0, pl.ds(at, n), from_y])
        else:
            ref = first_recv.at[way, step - 1, pl.ds(at, n)]
            arrived(("f", way, step, low, 0), ref, ref)

    def keep(post, z_from, block):
        post[pl.ds(pl.multiple_of(z_from * 32, 32), 32), :] = block.reshape(32, GATE)

    def first_step(step):
        for index in range(PARTS):
            for way in (0, 1):
                onward = first_ranges(way, step + 1)
                if index < len(onward):
                    low, high = onward[index]
                    for a, b in first_ranges(way, step):
                        if a <= high + 1 and b >= low + 1:
                            first_wait(way, step, a, b)
                    first_pass(way, step + 1, low, high)
        for way in (0, 1):
            if step <= first_n[way]:
                for a, b in first_ranges(way, step):
                    first_wait(way, step, a, b)
                z_from = lax.rem(z + NZ - step, NZ) if way == 0 else lax.rem(z + step, NZ)
                keep(first_post, z_from, first_recv[way, step - 1, first_start(way, 0, 0)])

    late_n = (15, 16)

    def late_own(way, phase, cross_y):
        left = late_n[way] - phase + 1
        to_y = 1 - y if cross_y else y
        at = z + left if way == 0 else z + NZ - left
        send(("l", way, phase, 0, cross_y), late_pre.at[at, to_y], late_recv.at[way, phase - 1, 0, y],
             g, near[way] * 2 + to_y)

    def late_pass(way, phase, low, high):
        n = high - low + 1
        send(("l", way, phase, low, 0), late_recv.at[way, phase - 2, pl.ds(low - 1, n)],
             late_recv.at[way, phase - 1, pl.ds(low, n)], g, near[way] * 2 + y)

    def late_ranges(phase):
        return list(reversed(ranges(1, phase - 1, PARTS))) if phase > 1 else []

    late_seen = set()

    def late_wait(way, phase, low, high):
        if (way, phase, low) in late_seen:
            return
        late_seen.add((way, phase, low))
        if low == 0:
            for cross_y in (0, 1):
                from_y = 1 - y if cross_y else y
                arrived(("l", way, phase, 0, cross_y), late_pre.at[0, 0], late_recv.at[way, phase - 1, 0, from_y])
        else:
            ref = late_recv.at[way, phase - 1, pl.ds(low, high - low + 1)]
            arrived(("l", way, phase, low, 0), ref, ref)

    def late_parts(phase):
        return [(0, 0)] + late_ranges(phase)

    def late_phase(phase):
        for way in (0, 1):
            if phase <= late_n[way]:
                for cross_y in (1, 0):
                    late_own(way, phase, cross_y)
        for index, (low, high) in enumerate(late_ranges(phase)):
            for way in (0, 1):
                if phase <= late_n[way]:
                    for a, b in late_parts(phase - 1):
                        if a <= high - 1 and b >= low - 1:
                            late_wait(way, phase - 1, a, b)
                    late_pass(way, phase, low, high)

    def beside(key, pre, post):
        send((key, "beside"), pre.at[z, 1 - y], post.at[pl.ds(pl.multiple_of((z * 2 + y) * 16, 16), 16)],
             g, z * 2 + 1 - y)
        post[pl.ds(pl.multiple_of((z * 2 + y) * 16, 16), 16), :] = pre[z, y]

    def beside_wait(key, pre, post):
        arrived((key, "beside"), pre.at[0, 0], post.at[pl.ds(pl.multiple_of((z * 2 + 1 - y) * 16, 16), 16)])

    def mix_send(which, source):
        def body(i, c):
            j = lax.rem(g + i, groups)
            pltpu.make_async_remote_copy(
                src_ref=source.at[pl.ds(j * 8, 8)], dst_ref=mix_in.at[which, g], send_sem=mix_s.at[which, 0, i],
                recv_sem=mix_r.at[which, 0, i], device_id=(j, q), device_id_type=MESH).start()
            return c
        lax.fori_loop(1, groups, body, 0)
        mix_in[which, g] = source[pl.ds(g * 8, 8)]

    def mix(which, target):
        def wait(i, c):
            j = lax.rem(g + groups - i, groups)
            pltpu.make_async_remote_copy(
                src_ref=target.at[pl.ds(0, 8)], dst_ref=mix_in.at[which, j], send_sem=mix_s.at[which, 0, i],
                recv_sem=mix_r.at[which, 0, i], device_id=(j, q), device_id_type=MESH).wait_recv()
            return c
        lax.fori_loop(1, groups, wait, 0)
        taken = mix_in.reshape(2 * 16 * 64, GATE)
        given = mix_out.reshape(2 * 16 * 64, GATE)
        low = [[(cross[0, 0, i, j], cross[0, 1, i, j]) for j in range(4)] for i in range(4)]
        high = [[(cross[1, 0, i, j], cross[1, 1, i, j]) for j in range(4)] for i in range(4)]

        def combine(matrix, vectors):
            out = []
            for i in range(4):
                re = im = None
                for j in range(4):
                    (cr, ci), (vr, vi) = matrix[i][j], vectors[j]
                    tr, ti = cr * vr - ci * vi, cr * vi + ci * vr
                    re, im = (tr, ti) if re is None else (re + tr, im + ti)
                out.append((re, im))
            return out

        def piece(n, c):
            def at(a, part):
                return pl.ds((which * 16 + a) * 64 + n * 16 + part, 8, stride=2)
            five = []
            for hi in range(4):
                five.append(combine(low, [(taken[at(hi * 4 + lo, 0), :], taken[at(hi * 4 + lo, 1), :])
                                          for lo in range(4)]))
            for lo in range(4):
                for hi, (re, im) in enumerate(combine(high, [five[h][lo] for h in range(4)])):
                    given[at(hi * 4 + lo, 0), :] = re
                    given[at(hi * 4 + lo, 1), :] = im
            return c
        lax.fori_loop(0, 4, piece, 0)

        def body(i, c):
            j = lax.rem(g + i, groups)
            pltpu.make_async_remote_copy(
                src_ref=mix_out.at[which, j], dst_ref=target.at[pl.ds(g * 8, 8)], send_sem=mix_s.at[which, 1, i],
                recv_sem=mix_r.at[which, 1, i], device_id=(j, q), device_id_type=MESH).start()
            return c
        lax.fori_loop(1, groups, body, 0)
        target[pl.ds(g * 8, 8)] = mix_out[which, g]

    def mix_wait(which, target):
        def wait(i, c):
            j = lax.rem(g + groups - i, groups)
            pltpu.make_async_remote_copy(
                src_ref=mix_out.at[which, 0], dst_ref=target.at[pl.ds(j * 8, 8)], send_sem=mix_s.at[which, 1, i],
                recv_sem=mix_r.at[which, 1, i], device_id=(j, q), device_id_type=MESH).wait_recv()
            return c
        lax.fori_loop(1, groups, wait, 0)

    def mix_done(which, target):
        def wait(i, c):
            for half in (0, 1):
                pltpu.make_async_remote_copy(
                    src_ref=mix_out.at[which, 0], dst_ref=mix_in.at[which, 0], send_sem=mix_s.at[which, half, i],
                    recv_sem=mix_r.at[which, half, i], device_id=(g, q), device_id_type=MESH).wait_send()
            return c
        lax.fori_loop(1, groups, wait, 0)

    load_gates.wait()
    real_form(0, 0)
    load_first.wait()
    for pair in pairs:
        value = high_gate(0, columns_of(first_x.reshape(*flat), pair))
        for base in (0, 1024):
            put(first_pre.reshape(2048, GATE), base, pair, value)
    pl.semaphore_wait(barrier, groups - 1 + 5)
    for index in range(PARTS):
        for cross_y in (1, 0):
            for way in (0, 1):
                first_own(way, *first_ranges(way, 1)[index], cross_y)
    load_late.wait()
    mix_send(0, late_x)
    beside("f", first_pre, first_post)
    real_form(1, 1)
    real_form(3, 2)
    turn[...] = jnp.dot(rep[2], rep[1], precision=HIGHEST, preferred_element_type=jnp.float32)
    real_form(2, 1)

    def late_before(pair):
        source = late_mixed.reshape(*flat)
        stacked = jnp.concatenate(
            [jnp.concatenate([rows(source, r, part) for part in (0, 1)], axis=1) for r in pair], axis=0)
        turned = low_gate(stacked)
        columns = jnp.concatenate(
            [jnp.concatenate([turned[i * GATE:(i + 1) * GATE, part * GATE:(part + 1) * GATE] for i in (0, 1)], axis=1)
             for part in (0, 1)], axis=0)
        value = high_gate(0, columns)
        for base in (0, 1024):
            put(late_pre.reshape(2048, GATE), base, pair, value)

    def first_after(pair):
        value = high_gate(1, columns_of(first_post, pair))
        stacked = jnp.concatenate(
            [jnp.concatenate([value[part * GATE:(part + 1) * GATE, i * GATE:(i + 1) * GATE] for part in (0, 1)], axis=1)
             for i in (0, 1)], axis=0)
        turned = low_gate(stacked)
        result = first_res.reshape(*flat)
        for i, r in enumerate(pair):
            for part in (0, 1):
                result[pl.ds(r * 2 + part, GATE, stride=8), :] = turned[
                    i * GATE:(i + 1) * GATE, part * GATE:(part + 1) * GATE]

    last = LATE_FROM + 16
    for tick in range(1, last + 1):
        if tick <= 16:
            first_step(tick)
        if tick > LATE_FROM:
            late_phase(tick - LATE_FROM)
        if tick == MIX_AT:
            mix(0, late_mixed)
        for i in (0, 1):
            if tick == TURN_AT[i]:
                if i == 0:
                    mix_wait(0, late_mixed)
                late_before(pairs[i])
        if tick == LATE_FROM:
            beside("l", late_pre, late_post)
        for i in (0, 1):
            if tick == BACK_AT[i]:
                if i == 0:
                    beside_wait("f", first_pre, first_post)
                first_after(pairs[i])
                if i == 1:
                    mix_send(1, first_res)
        if tick == BACK_MIX_AT:
            mix(1, first_out)

    mix_wait(1, first_out)
    store_first = pltpu.make_async_copy(first_out, out_ref.at[:, pl.ds(0, 8), :], local_sem.at[3])
    store_first.start()

    beside_wait("l", late_pre, late_post)
    for way in (0, 1):
        n = late_n[way]
        for a, b in late_parts(n):
            late_wait(way, n, a, b)
        for k in range(n):
            z_from = lax.rem(z + NZ - k - 1, NZ) if way == 0 else lax.rem(z + k + 1, NZ)
            keep(late_post, z_from, late_recv[way, n - 1, k])
    for pair in pairs:
        put(late_out.reshape(*flat), 0, pair, high_gate(1, columns_of(late_post, pair)))
    store_late = pltpu.make_async_copy(late_out, out_ref.at[:, pl.ds(8, 8), :], local_sem.at[4])
    store_late.start()

    for copy in sent:
        copy.wait_send()
    mix_done(0, late_mixed)
    mix_done(1, first_out)
    store_first.wait()
    store_late.wait()


def on_device(amplitudes, layer_gates, cross_gates):
    groups = lax.axis_size("grp")
    view = amplitudes.reshape(2, 1024, GATE).transpose(1, 0, 2).reshape(GATE, 16, GATE)
    vm = lambda *shape: pltpu.VMEM(shape, jnp.float32)
    result = pl.pallas_call(
        functools.partial(kernel, groups),
        out_shape=jax.ShapeDtypeStruct((GATE, 16, GATE), jnp.float32),
        in_specs=[pl.BlockSpec(memory_space=pl.ANY), pl.BlockSpec(memory_space=pl.ANY),
                  pl.BlockSpec(memory_space=pltpu.SMEM)],
        out_specs=pl.BlockSpec(memory_space=pl.ANY),
        scratch_shapes=[
            vm(GATE, 8, GATE), vm(GATE, 8, GATE), vm(4, 2, GATE, GATE), vm(3, 256, 256), vm(256, 256),
            vm(64, 2, 16, GATE), vm(64, 2, 16, GATE), vm(2, 16, 16, 2, 16, GATE), vm(2, 16, 16, 2, 16, GATE),
            vm(1024, GATE), vm(1024, GATE), vm(GATE, 8, GATE), vm(GATE, 8, GATE), vm(GATE, 8, GATE), vm(GATE, 8, GATE),
            vm(2, 16, 8, 8, GATE), vm(2, 16, 8, 8, GATE),
            pltpu.SemaphoreType.DMA((272,)), pltpu.SemaphoreType.DMA((272,)),
            pltpu.SemaphoreType.DMA((2, 2, 16)), pltpu.SemaphoreType.DMA((2, 2, 16)),
            pltpu.SemaphoreType.DMA((5,)),
        ],
        compiler_params=pltpu.CompilerParams(collective_id=0, has_side_effects=True,
                                             vmem_limit_bytes=60 * 1024 * 1024),
    )(view, layer_gates, cross_gates)
    return result.reshape(1024, 2, GATE).transpose(1, 0, 2).reshape(2, -1)


def solution(mesh):
    return jax.shard_map(
        on_device,
        mesh=mesh,
        in_specs=(P(None, ("grp", "qb")), P(), P()),
        out_specs=P(None, ("grp", "qb")),
        check_vma=False,
    )
```

```python
import functools

import jax
import jax.numpy as jnp
from jax import lax
from jax.experimental import pallas as pl
from jax.experimental.pallas import tpu as pltpu
from jax.sharding import PartitionSpec as P

MESH = pl.DeviceIdType.MESH
GATE = 128
NZ = 32
PARTS = 4
MIX_AT = 2
TURN_AT = (4, 5)
LATE_FROM = 7
BACK_AT = (17, 18)
BACK_MIX_AT = 21
MESSAGES = 257
HIGHEST = lax.Precision.HIGHEST


def ranges(low, high, parts):
    count = high - low + 1
    parts = min(parts, count)
    edges = [low + count * i // parts for i in range(parts + 1)]
    return [(edges[i], edges[i + 1] - 1) for i in reversed(range(parts))]


def kernel(groups, x_hbm, gates_hbm, cross, out_ref, first_x, late_x, gates, rep, turn,
           first_pre, late_pre, late_src, first_recv, late_recv, first_post, late_post, first_res, late_mixed, first_out, late_out,
           mix_in, mix_out, ssem, rsem, mix_s, mix_r, local_sem):
    g = lax.axis_index("grp")
    q = lax.axis_index("qb")
    z, y = q // 2, q % 2
    up, down = lax.rem(z + 1, NZ), lax.rem(z + NZ - 1, NZ)
    near = (up, down)

    barrier = pltpu.get_barrier_semaphore()

    def greet(to_g, to_q):
        pl.semaphore_signal(barrier, inc=1, device_id=(to_g, to_q), device_id_type=MESH)

    for zz in near:
        for yy in (0, 1):
            greet(g, zz * 2 + yy)
    greet(g, z * 2 + 1 - y)

    def greet_group(i, c):
        greet(lax.rem(g + i, groups), q)
        return c

    lax.fori_loop(1, groups, greet_group, 0)

    load_gates = [pltpu.make_async_copy(gates_hbm.at[i], gates.at[i], local_sem.at[5 + i]) for i in range(4)]
    load_first = pltpu.make_async_copy(x_hbm.at[:, pl.ds(0, 8), :], first_x, local_sem.at[1])
    load_late = pltpu.make_async_copy(x_hbm.at[:, pl.ds(8, 8), :], late_x, local_sem.at[2])
    load_first.start()
    load_gates[0].start()
    load_late.start()
    for i in (1, 3, 2):
        load_gates[i].start()

    def real_form(index, place):
        re, im = gates[index, 0], gates[index, 1]
        rep[place, 0:GATE, 0:GATE] = re
        rep[place, 0:GATE, GATE:] = -im
        rep[place, GATE:, 0:GATE] = im
        rep[place, GATE:, GATE:] = re

    def rows(ref, r, part):
        return ref[pl.ds(r * 2 + part, GATE, stride=8), :]

    def high_gate(place, columns):
        return jnp.dot(rep[place], columns, precision=HIGHEST, preferred_element_type=jnp.float32)

    def low_gate(stacked):
        return lax.dot_general(stacked, turn[...], (((1,), (1,)), ((), ())), precision=HIGHEST,
                               preferred_element_type=jnp.float32)

    def columns_of(ref, pair):
        return jnp.concatenate(
            [jnp.concatenate([rows(ref, r, part) for r in pair], axis=1) for part in (0, 1)], axis=0)

    def put(ref, base, pair, value):
        for i, r in enumerate(pair):
            for part in (0, 1):
                ref[pl.ds(base + r * 2 + part, GATE, stride=8), :] = value[
                    part * GATE:(part + 1) * GATE, i * GATE:(i + 1) * GATE]

    flat = (1024, GATE)
    pairs = ((0, 1), (2, 3))

    sems = {}

    def sem_of(key):
        return sems.setdefault(key, len(sems))

    kinds = ("f", "l", "fy", "ly")

    def send(key, src, dst, to_g, to_q):
        pltpu.make_async_remote_copy(src_ref=src, dst_ref=dst, send_sem=ssem.at[kinds.index(key[0])],
                                     recv_sem=rsem.at[sem_of(key)], device_id=(to_g, to_q),
                                     device_id_type=MESH).start()

    def sent(kind, like):
        pltpu.make_async_remote_copy(src_ref=like, dst_ref=like, send_sem=ssem.at[kinds.index(kind)],
                                     recv_sem=rsem.at[0], device_id=(g, q), device_id_type=MESH).wait_send()

    def arrived(key, src, dst):
        pltpu.make_async_remote_copy(src_ref=src, dst_ref=dst, send_sem=ssem.at[0], recv_sem=rsem.at[sem_of(key)],
                                     device_id=(g, q), device_id_type=MESH).wait_recv()

    first_n = (16, 15)

    def first_start(way, low, high):
        return low if way == 0 else 15 - high

    def first_own(way, low, high, cross_y):
        n = high - low + 1
        to_y = 1 - y if cross_y else y
        at = z + low + 1 if way == 0 else z + NZ - high - 1
        send(("f", way, 1, low, cross_y), first_pre.at[pl.ds(at, n), to_y],
             first_recv.at[way, 0, pl.ds(first_start(way, low, high), n), y], g, near[way] * 2 + to_y)

    def first_pass(way, step, low, high):
        n = high - low + 1
        send(("f", way, step, low, 0), first_recv.at[way, step - 2, pl.ds(first_start(way, low + 1, high + 1), n)],
             first_recv.at[way, step - 1, pl.ds(first_start(way, low, high), n)], g, near[way] * 2 + y)

    def first_ranges(way, step):
        return ranges(0, first_n[way] - step, PARTS) if step <= first_n[way] else []

    first_seen = set()

    def first_wait(way, step, low, high):
        if (way, step, low) in first_seen:
            return
        first_seen.add((way, step, low))
        n = high - low + 1
        at = first_start(way, low, high)
        if step == 1:
            for cross_y in (0, 1):
                from_y = 1 - y if cross_y else y
                arrived(("f", way, 1, low, cross_y), first_pre.at[pl.ds(0, n), 0],
                        first_recv.at[way, 0, pl.ds(at, n), from_y])
        else:
            ref = first_recv.at[way, step - 1, pl.ds(at, n)]
            arrived(("f", way, step, low, 0), ref, ref)

    def keep(post, z_from, block):
        post[pl.ds(pl.multiple_of(z_from * 32, 32), 32), :] = block.reshape(32, GATE)

    def first_step(step):
        for index in range(PARTS):
            for way in (0, 1):
                onward = first_ranges(way, step + 1)
                if index < len(onward):
                    low, high = onward[index]
                    for a, b in first_ranges(way, step):
                        if a <= high + 1 and b >= low + 1:
                            first_wait(way, step, a, b)
                    first_pass(way, step + 1, low, high)
        for way in (0, 1):
            if step <= first_n[way]:
                for a, b in first_ranges(way, step):
                    first_wait(way, step, a, b)
                z_from = lax.rem(z + NZ - step, NZ) if way == 0 else lax.rem(z + step, NZ)
                keep(first_post, z_from, first_recv[way, step - 1, first_start(way, 0, 0)])

    late_n = (15, 16)

    def late_own(way, phase):
        left = late_n[way] - phase + 1
        at = lax.rem(z + left, NZ) if way == 0 else lax.rem(z + NZ - left, NZ)
        send(("l", way, phase, 0), late_src.at[at], late_recv.at[way, phase - 1, 0], g, near[way] * 2 + y)

    def late_pass(way, phase, low, high):
        n = high - low + 1
        send(("l", way, phase, low), late_recv.at[way, phase - 2, pl.ds(low - 1, n)],
             late_recv.at[way, phase - 1, pl.ds(low, n)], g, near[way] * 2 + y)

    def late_ranges(phase):
        return list(reversed(ranges(1, phase - 1, PARTS))) if phase > 1 else []

    late_seen = set()

    def late_wait(way, phase, low, high):
        if (way, phase, low) in late_seen:
            return
        late_seen.add((way, phase, low))
        ref = late_recv.at[way, phase - 1, pl.ds(low, high - low + 1)]
        arrived(("l", way, phase, low), ref, ref)

    def late_parts(phase):
        return [(0, 0)] + late_ranges(phase)

    def late_phase(phase):
        for way in (0, 1):
            if phase <= late_n[way]:
                late_own(way, phase)
        for index, (low, high) in enumerate(late_ranges(phase)):
            for way in (0, 1):
                if phase <= late_n[way]:
                    for a, b in late_parts(phase - 1):
                        if a <= high - 1 and b >= low - 1:
                            late_wait(way, phase - 1, a, b)
                    late_pass(way, phase, low, high)

    def first_beside():
        send(("fy",), first_pre.at[z, 1 - y], first_post.at[pl.ds(pl.multiple_of((z * 2 + y) * 16, 16), 16)],
             g, z * 2 + 1 - y)
        first_post[pl.ds(pl.multiple_of((z * 2 + y) * 16, 16), 16), :] = first_pre[z, y]

    def first_beside_wait():
        arrived(("fy",), first_pre.at[0, 0], first_post.at[pl.ds(pl.multiple_of((z * 2 + 1 - y) * 16, 16), 16)])

    def late_beside():
        send(("ly",), late_pre.at[:, 1 - y], late_src.at[:, y], g, z * 2 + 1 - y)
        late_src[:, y] = late_pre[:, y]

    def late_beside_wait():
        arrived(("ly",), late_pre.at[:, 0], late_src.at[:, 1 - y])
        keep(late_post, z, late_src[z])

    def mix_send(which, source):
        def body(i, c):
            j = lax.rem(g + i, groups)
            pltpu.make_async_remote_copy(
                src_ref=source.at[pl.ds(j * 8, 8)], dst_ref=mix_in.at[which, g], send_sem=mix_s.at[which, 0],
                recv_sem=mix_r.at[which, 0], device_id=(j, q), device_id_type=MESH).start()
            return c
        lax.fori_loop(1, groups, body, 0)
        mix_in[which, g] = source[pl.ds(g * 8, 8)]

    def mix_copy(which, half):
        others = mix_in.at[which, pl.ds(0, groups - 1)]
        return pltpu.make_async_remote_copy(
            src_ref=others, dst_ref=others, send_sem=mix_s.at[which, half], recv_sem=mix_r.at[which, half],
            device_id=(g, q), device_id_type=MESH)

    def mix_arrived(which, half):
        mix_copy(which, half).wait_recv()

    def mix_sent(which, half):
        mix_copy(which, half).wait_send()

    def mix(which, target):
        mix_arrived(which, 0)
        taken = mix_in.reshape(2 * 16 * 64, GATE)
        given = mix_out.reshape(2 * 16 * 64, GATE)
        low = [[(cross[0, 0, i, j], cross[0, 1, i, j]) for j in range(4)] for i in range(4)]
        high = [[(cross[1, 0, i, j], cross[1, 1, i, j]) for j in range(4)] for i in range(4)]

        def combine(matrix, vectors):
            out = []
            for i in range(4):
                re = im = None
                for j in range(4):
                    (cr, ci), (vr, vi) = matrix[i][j], vectors[j]
                    tr, ti = cr * vr - ci * vi, cr * vi + ci * vr
                    re, im = (tr, ti) if re is None else (re + tr, im + ti)
                out.append((re, im))
            return out

        def piece(n, c):
            def at(a, part):
                return pl.ds((which * 16 + a) * 64 + n * 16 + part, 8, stride=2)
            five = []
            for hi in range(4):
                five.append(combine(low, [(taken[at(hi * 4 + lo, 0), :], taken[at(hi * 4 + lo, 1), :])
                                          for lo in range(4)]))
            for lo in range(4):
                for hi, (re, im) in enumerate(combine(high, [five[h][lo] for h in range(4)])):
                    given[at(hi * 4 + lo, 0), :] = re
                    given[at(hi * 4 + lo, 1), :] = im
            return c
        lax.fori_loop(0, 4, piece, 0)

        def body(i, c):
            j = lax.rem(g + i, groups)
            pltpu.make_async_remote_copy(
                src_ref=mix_out.at[which, j], dst_ref=target.at[pl.ds(g * 8, 8)], send_sem=mix_s.at[which, 1],
                recv_sem=mix_r.at[which, 1], device_id=(j, q), device_id_type=MESH).start()
            return c
        lax.fori_loop(1, groups, body, 0)
        target[pl.ds(g * 8, 8)] = mix_out[which, g]

    load_gates[0].wait()
    real_form(0, 0)
    load_first.wait()
    for pair in pairs:
        value = high_gate(0, columns_of(first_x.reshape(*flat), pair))
        for base in (0, 1024):
            put(first_pre.reshape(2048, GATE), base, pair, value)
    pl.semaphore_wait(barrier, groups - 1 + 5)
    for index in range(PARTS):
        for cross_y in (1, 0):
            for way in (0, 1):
                first_own(way, *first_ranges(way, 1)[index], cross_y)
    load_late.wait()
    mix_send(0, late_x)
    first_beside()
    for i in (1, 3, 2):
        load_gates[i].wait()
    real_form(1, 1)
    real_form(3, 2)
    turn[...] = jnp.dot(rep[2], rep[1], precision=HIGHEST, preferred_element_type=jnp.float32)
    real_form(2, 1)

    def late_before(pair):
        source = late_mixed.reshape(*flat)
        stacked = jnp.concatenate(
            [jnp.concatenate([rows(source, r, part) for part in (0, 1)], axis=1) for r in pair], axis=0)
        turned = low_gate(stacked)
        columns = jnp.concatenate(
            [jnp.concatenate([turned[i * GATE:(i + 1) * GATE, part * GATE:(part + 1) * GATE] for i in (0, 1)], axis=1)
             for part in (0, 1)], axis=0)
        put(late_pre.reshape(*flat), 0, pair, high_gate(0, columns))

    def first_after(pair):
        value = high_gate(1, columns_of(first_post, pair))
        stacked = jnp.concatenate(
            [jnp.concatenate([value[part * GATE:(part + 1) * GATE, i * GATE:(i + 1) * GATE] for part in (0, 1)], axis=1)
             for i in (0, 1)], axis=0)
        turned = low_gate(stacked)
        result = first_res.reshape(*flat)
        for i, r in enumerate(pair):
            for part in (0, 1):
                result[pl.ds(r * 2 + part, GATE, stride=8), :] = turned[
                    i * GATE:(i + 1) * GATE, part * GATE:(part + 1) * GATE]

    last = LATE_FROM + 16
    for tick in range(1, last + 1):
        if tick <= 16:
            first_step(tick)
        if tick > LATE_FROM:
            late_phase(tick - LATE_FROM)
        if tick == MIX_AT:
            mix(0, late_mixed)
        for i in (0, 1):
            if tick == TURN_AT[i]:
                if i == 0:
                    mix_arrived(0, 1)
                late_before(pairs[i])
        if tick == TURN_AT[1]:
            late_beside()
        if tick == LATE_FROM:
            late_beside_wait()
        for i in (0, 1):
            if tick == BACK_AT[i]:
                if i == 0:
                    first_beside_wait()
                first_after(pairs[i])
                if i == 1:
                    mix_send(1, first_res)
        if tick == BACK_MIX_AT:
            mix(1, first_out)

    mix_arrived(1, 1)
    store_first = pltpu.make_async_copy(first_out, out_ref.at[:, pl.ds(0, 8), :], local_sem.at[3])
    store_first.start()

    for way in (0, 1):
        n = late_n[way]
        for a, b in late_parts(n):
            late_wait(way, n, a, b)
        for k in range(n):
            z_from = lax.rem(z + NZ - k - 1, NZ) if way == 0 else lax.rem(z + k + 1, NZ)
            keep(late_post, z_from, late_recv[way, n - 1, k])
    for pair in pairs:
        put(late_out.reshape(*flat), 0, pair, high_gate(1, columns_of(late_post, pair)))
    store_late = pltpu.make_async_copy(late_out, out_ref.at[:, pl.ds(8, 8), :], local_sem.at[4])
    store_late.start()

    assert len(sems) <= MESSAGES, len(sems)
    sent("f", first_recv.at[0])
    sent("l", late_recv.at[0])
    sent("fy", first_pre.at[0, 0])
    sent("ly", late_pre.at[:, 0])
    for which in (0, 1):
        for half in (0, 1):
            mix_sent(which, half)
    store_first.wait()
    store_late.wait()


def on_device(amplitudes, layer_gates, cross_gates):
    groups = lax.axis_size("grp")
    view = amplitudes.reshape(2, 1024, GATE).transpose(1, 0, 2).reshape(GATE, 16, GATE)
    vm = lambda *shape: pltpu.VMEM(shape, jnp.float32)
    result = pl.pallas_call(
        functools.partial(kernel, groups),
        out_shape=jax.ShapeDtypeStruct((GATE, 16, GATE), jnp.float32),
        in_specs=[pl.BlockSpec(memory_space=pl.ANY), pl.BlockSpec(memory_space=pl.ANY),
                  pl.BlockSpec(memory_space=pltpu.SMEM)],
        out_specs=pl.BlockSpec(memory_space=pl.ANY),
        scratch_shapes=[
            vm(GATE, 8, GATE), vm(GATE, 8, GATE), vm(4, 2, GATE, GATE), vm(3, 256, 256), vm(256, 256),
            vm(2 * NZ, 2, 16, GATE), vm(NZ, 2, 16, GATE), vm(NZ, 2, 16, GATE), vm(2, 16, 16, 2, 16, GATE), vm(2, 16, 16, 2, 16, GATE),
            vm(1024, GATE), vm(1024, GATE), vm(GATE, 8, GATE), vm(GATE, 8, GATE), vm(GATE, 8, GATE), vm(GATE, 8, GATE),
            vm(2, 16, 8, 8, GATE), vm(2, 16, 8, 8, GATE),
            pltpu.SemaphoreType.DMA((4,)), pltpu.SemaphoreType.DMA((MESSAGES,)),
            pltpu.SemaphoreType.DMA((2, 2)), pltpu.SemaphoreType.DMA((2, 2)),
            pltpu.SemaphoreType.DMA((9,)),
        ],
        compiler_params=pltpu.CompilerParams(collective_id=0, has_side_effects=True,
                                             vmem_limit_bytes=60 * 1024 * 1024),
    )(view, layer_gates, cross_gates)
    return result.reshape(1024, 2, GATE).transpose(1, 0, 2).reshape(2, -1)


def solution(mesh):
    return jax.shard_map(
        on_device,
        mesh=mesh,
        in_specs=(P(None, ("grp", "qb")), P(), P()),
        out_specs=P(None, ("grp", "qb")),
        check_vma=False,
    )
```
